512 devices in a mesh: pole: 16 (over z_lo, x), dom: 32 (over y, z_hi, core).
Axes of the slice: x: 4, y: 8, z: 8 (z_hi: 2, z_lo: 4; z = z_hi * 4 + z_lo), core: 2. Of those that a mesh axis runs over, the one named last changes fastest.
Arguments:
- y_interior: float32 [32, 512, 256], P('dom', 'pole'), may hold values from -6 to 6
- y_separator: float32 [32, 64, 256], P('dom'), may hold values from -6 to 6
- green: float32 [2, 16, 32, 512, 512], P(None, 'pole', 'dom'), as said below
- pole_data: float32 [4, 16], P(None, 'pole'), as said below
- coupling: float32 [32, 2, 64, 128], P('dom')
- sep_block: float32 [32, 64, 64], P('dom'), as said below
- iface_rows: int32 [32, 2, 128], P('dom'), may hold values from 0 to 511, as said below
Outputs:
- filtered: float32 [32, 512, 256], P('dom', 'pole')
- filtered_sep: float32 [32, 64, 256], P('dom', 'pole')
The draws below stay inside these ranges and needn't reach their ends.
Inputs may be any that keep to these rules, and one draw needn't show every extreme that they name: green[:, p, d] holds the real and imaginary parts of the inverse of z[p] I - H[d], where H[d] is a real symmetric matrix of order 512 and z[p] is the pole of pole_data. `pole_data`: every pole lies in the upper half plane with imaginary part 0.3 or more. `sep_block`: each block is symmetric. iface_rows[d, 0] and iface_rows[d, 1] each list 128 distinct rows of domain d, and no row is in both.
All inputs are finite; a program needn't handle non-finite values.
Results may differ from the reference program's by a relative error of at most 0.00095.
Values sent between devices are 32-bit elements; how exact they have to be, the bound alone decides.
No kernel may reach another device: no remote copies, remote signals or barrier semaphores. Data moves between devices by JAX's collectives and lax.ppermute only.
A program may use at most 64 MiB of HBM per device.

```python
import math
import jax
import jax.numpy as jnp
from jax import lax

NI = 512
S = 64
B = 128
M = 256
POLES = 16
DOMAINS = 32


dimer_hop = 24.0


edge_spread = 0.5


bulk_link = 0.5


couple_gain = 12.0


def pole_table(key):
    pole_key = jax.random.fold_in(key, 101)
    pole_keys = jax.random.split(pole_key, 4)
    center = jax.random.uniform(pole_keys[0], (), jnp.float32, -0.4, 0.4)
    radius = jax.random.uniform(pole_keys[1], (), jnp.float32, 1.3, 1.7)
    height = radius * jax.random.uniform(pole_keys[2], (), jnp.float32, 0.8, 1.2)
    spacing = 0.76 * math.pi / POLES
    jitter = jax.random.uniform(pole_keys[3], (POLES,), jnp.float32, 0.2, 0.8)
    angles = 0.12 * math.pi + spacing * (jnp.arange(POLES, dtype=jnp.float32) + jitter)
    real_part = center + radius * jnp.cos(angles)
    imag_part = height * jnp.sin(angles)
    weight_real = spacing / math.pi * height * jnp.cos(angles)
    weight_imag = spacing / math.pi * radius * jnp.sin(angles)
    return jnp.stack([real_part, imag_part, weight_real, weight_imag])


def iface_ranking(key):
    row_key = jax.random.fold_in(key, 404)
    positions = jnp.arange(NI, dtype=jnp.int32)[None, :]
    domain_ids = jnp.arange(DOMAINS, dtype=jnp.int32)[:, None]
    scores = jax.random.randint(row_key, (DOMAINS, NI), 0, 1 << 20, dtype=jnp.int32) * NI + positions
    end_rows = (positions == 0) | (positions == NI - 1)
    scores = jnp.where((domain_ids == 0) & end_rows, -1 - positions, scores)
    scores = jnp.where((domain_ids == 1) & end_rows, (1 << 30) + positions, scores)
    return jnp.argsort(scores, axis=1).astype(jnp.int32)


def draw_pole_data(key, part):
    return pole_table(key)


def draw_green(key, part):
    pole_rows = pole_table(key)
    ranking = iface_ranking(key)
    matrix_key = jax.random.fold_in(key, 202)
    noise_draw = jax.random.normal(matrix_key, (DOMAINS, NI, NI), jnp.float32)
    symmetric = (noise_draw + jnp.swapaxes(noise_draw, 1, 2)) / jnp.sqrt(2.0)
    positions = jnp.arange(NI, dtype=jnp.int32)
    in_first = positions < B
    in_last = positions >= NI - B
    in_edge = in_first | in_last
    in_bulk = jnp.logical_not(in_edge)
    edge_scale = edge_spread / math.sqrt(B)
    bulk_scale = 1.0 / math.sqrt(max(NI - 2 * B, 1))
    link_scale = bulk_link / math.sqrt(NI)
    same_side = in_first[:, None] & in_first[None, :] | in_last[:, None] & in_last[None, :]
    both_bulk = in_bulk[:, None] & in_bulk[None, :]
    mixed = in_edge[:, None] & in_bulk[None, :] | in_bulk[:, None] & in_edge[None, :]
    scale_table = (jnp.where(same_side, edge_scale, 0.0) + jnp.where(both_bulk, bulk_scale, 0.0) + jnp.where(mixed, link_scale, 0.0)).astype(jnp.float32)
    paired = (positions[None, :] == positions[:, None] + (NI - B)) & in_first[:, None]
    dimer = jnp.where(paired | paired.T, dimer_hop, 0.0).astype(jnp.float32)
    canonical = symmetric * scale_table[None] + dimer[None]
    eigen_values, canon_vectors = jnp.linalg.eigh(canonical)
    inverse = jnp.argsort(ranking, axis=1).astype(jnp.int32)
    eigen_vectors = jnp.take_along_axis(canon_vectors, inverse[:, :, None], axis=1)
    offset = pole_rows[0][:, None, None] - eigen_values[None]
    denominator = offset * offset + pole_rows[1][:, None, None] ** 2
    real_weight = offset / denominator
    imag_weight = -pole_rows[1][:, None, None] / denominator
    green_real = jnp.einsum('dik,pdk,djk->pdij', eigen_vectors, real_weight, eigen_vectors)
    green_imag = jnp.einsum('dik,pdk,djk->pdij', eigen_vectors, imag_weight, eigen_vectors)
    return jnp.stack([green_real, green_imag]).astype(jnp.float32)


def draw_coupling(key, part):
    couple_key = jax.random.fold_in(key, 505)
    values = jax.random.normal(couple_key, (DOMAINS, 2, S, B), jnp.float32)
    return (values * (couple_gain / math.sqrt(B))).astype(jnp.float32)


def draw_sep_block(key, part):
    block_key = jax.random.fold_in(key, 303)
    noise_draw = jax.random.normal(block_key, (DOMAINS, S, S), jnp.float32)
    return (noise_draw + jnp.swapaxes(noise_draw, 1, 2)) / jnp.sqrt(2.0 * S)


def draw_iface_rows(key, part):
    ranking = iface_ranking(key)
    return jnp.stack([ranking[:, :B], ranking[:, NI - B:]], axis=1).astype(jnp.int32)


def steps_of(own_key, dims, cuts, smallest, top_value):
    gain = 1.0
    for dim, blocks in cuts:
        draws = jax.random.uniform(jax.random.fold_in(jax.random.fold_in(own_key, 6), dim), (blocks,), jnp.float32, smallest / len(cuts), top_value / len(cuts))
        gain = gain * jnp.repeat(jnp.exp(draws), dims[dim] // blocks).reshape((-1,) + (1,) * (len(dims) - 1 - dim))
    return gain


def noise(key, extent, scale, most, cuts=(), kind=jnp.bfloat16):
    array = scale * jax.random.normal(key, extent, jnp.float32)
    if cuts:
        array = array * steps_of(key, extent, cuts, -0.22, 0.18)
    return jnp.clip(array, -most, most).astype(kind)


def setup_inputs(seed: int = 0) -> dict:
    streams_of = jax.random.split(jax.random.key(seed), 8)
    return {
        "y_interior": noise(streams_of[0], (DOMAINS, NI, M), 1.0, 6.0, ((0, 32), (1, 16)), jnp.float32),
        "y_separator": noise(streams_of[1], (DOMAINS, S, M), 1.0, 6.0, ((0, 32),), jnp.float32),
        "green": draw_green(jax.random.fold_in(streams_of[7], 71), 0),
        "pole_data": draw_pole_data(jax.random.fold_in(streams_of[7], 71), 0),
        "coupling": draw_coupling(jax.random.fold_in(streams_of[7], 71), 0),
        "sep_block": draw_sep_block(jax.random.fold_in(streams_of[7], 71), 0),
        "iface_rows": draw_iface_rows(jax.random.fold_in(streams_of[7], 71), 0),
    }


precise_mode = lax.Precision.HIGHEST

def matmul(left_side, right_side):
    return jnp.matmul(left_side, right_side, precision=precise_mode)

def complex_mul(left_factor, right_factor):
    return jnp.stack([matmul(left_factor[0], right_factor[0]) - matmul(left_factor[1], right_factor[1]), matmul(left_factor[0], right_factor[1]) + matmul(left_factor[1], right_factor[0])])

def real_left(real_mat, right_factor):
    return jnp.stack([matmul(real_mat, right_factor[0]), matmul(real_mat, right_factor[1])])

def real_right(left_factor, real_mat):
    return jnp.stack([matmul(left_factor[0], real_mat), matmul(left_factor[1], real_mat)])

def complex_solve(pivot_blk, right_hand):
    sep_order = pivot_blk.shape[-1]
    upper_half = jnp.concatenate([pivot_blk[0], -pivot_blk[1]], axis=1)
    lower_half = jnp.concatenate([pivot_blk[1], pivot_blk[0]], axis=1)
    system = jnp.concatenate([upper_half, lower_half], axis=0)
    stacked = jnp.concatenate([right_hand[0], right_hand[1]], axis=0)
    normal_matrix = matmul(system.T, system)
    factor = jnp.linalg.cholesky(normal_matrix)
    solved = jax.scipy.linalg.cho_solve((factor, True), matmul(system.T, stacked))
    return jnp.stack([solved[:sep_order], solved[sep_order:]])

def chain_solve(pivots, lowers, uppers, rights):
    sep_width = pivots.shape[-1]

    def forward(carry, chain_items):
        prev_coupled, prev_partial = carry
        pivot_blk, lower_blk, upper_blk, right_blk = chain_items
        reduced = pivot_blk - complex_mul(lower_blk, prev_coupled)
        adjusted = right_blk - complex_mul(lower_blk, prev_partial)
        solved = complex_solve(reduced, jnp.concatenate([upper_blk, adjusted], axis=-1))
        result = (solved[:, :, :sep_width], solved[:, :, sep_width:])
        return (result, result)
    initial = (jnp.zeros(pivots.shape[1:], jnp.float32), jnp.zeros(rights.shape[1:], jnp.float32))
    unused, (coupled, partial_sol) = lax.scan(forward, initial, (pivots, lowers, uppers, rights))

    def backward(following, chain_items):
        coupled_blk, partial_blk = chain_items
        current = partial_blk - complex_mul(coupled_blk, following)
        return (current, current)
    unused_last, solutions = lax.scan(backward, jnp.zeros(rights.shape[1:], jnp.float32), (coupled, partial_sol), reverse=True)
    return solutions

def domain_pieces(green_dom, interior_v, coupling_dom, rows_dom):
    right_rows = rows_dom[0]
    left_rows = rows_dom[1]
    right_map = coupling_dom[0]
    left_map = coupling_dom[1]
    inner_u = real_right(jnp.take(green_dom, right_rows, axis=2), right_map.T)
    inner_w = real_right(jnp.take(green_dom, left_rows, axis=2), left_map.T)
    own_pivot = real_left(right_map, jnp.take(inner_u, right_rows, axis=1))
    own_lower = -real_left(right_map, jnp.take(inner_w, right_rows, axis=1))
    own_right = real_left(right_map, jnp.take(interior_v, right_rows, axis=1))
    next_pack = jnp.concatenate([real_left(left_map, jnp.take(inner_w, left_rows, axis=1)), real_left(left_map, jnp.take(inner_u, left_rows, axis=1)), real_left(left_map, jnp.take(interior_v, left_rows, axis=1))], axis=-1)
    return (inner_u, inner_w, own_pivot, own_lower, own_right, next_pack)

def reference(y_interior, y_separator, green, pole_data, coupling, sep_block, iface_rows):
    domains = y_interior.shape[0]
    poles = pole_data.shape[1]
    sep_order = sep_block.shape[-1]
    identity = jnp.eye(sep_order, dtype=jnp.float32)
    not_first = (jnp.arange(domains, dtype=jnp.int32) > 0).astype(jnp.float32)[:, None, None, None]
    separator_rhs = jnp.stack([y_separator, jnp.zeros_like(y_separator)], axis=1)
    separator_own = jnp.stack([sep_block, jnp.zeros_like(sep_block)], axis=1)

    def per_pole(totals, pole_index):
        column = pole_data[:, pole_index]

        def per_domain(domain_index):
            green_dom = green[:, pole_index, domain_index]
            interior_v = real_right(green_dom, y_interior[domain_index])
            return (interior_v,) + domain_pieces(green_dom, interior_v, coupling[domain_index], iface_rows[domain_index])
        interior_v, inner_u, inner_w, own_pivot, own_lower, own_right, next_pack = lax.map(per_domain, jnp.arange(domains, dtype=jnp.int32))
        shifted = jnp.concatenate([next_pack[1:], jnp.zeros_like(next_pack[:1])], axis=0)
        shift_eye = jnp.stack([column[0] * identity, column[1] * identity])
        pivots = shift_eye[None] - separator_own - own_pivot - shifted[..., :sep_order]
        uppers = -shifted[..., sep_order:2 * sep_order]
        rights = separator_rhs + own_right + shifted[..., 2 * sep_order:]
        lowers = own_lower * not_first
        solutions = chain_solve(pivots, lowers, uppers, rights)
        previous = jnp.concatenate([jnp.zeros_like(solutions[:1]), solutions[:-1]], axis=0)
        field_value = interior_v + jax.vmap(complex_mul)(inner_u, solutions) + jax.vmap(complex_mul)(inner_w, previous)
        weighted = column[2] * field_value[:, 0] - column[3] * field_value[:, 1]
        weighted_sep = column[2] * solutions[:, 0] - column[3] * solutions[:, 1]
        return ((totals[0] + weighted, totals[1] + weighted_sep), None)
    initial = (jnp.zeros(y_interior.shape, jnp.float32), jnp.zeros(y_separator.shape, jnp.float32))
    (filtered, filtered_sep), unused = lax.scan(per_pole, initial, jnp.arange(poles, dtype=jnp.int32))
    return (filtered, filtered_sep)
```

```python
import jax
import jax.numpy as jnp
from jax import lax
from jax.experimental import pallas as pl
from jax.experimental.pallas import tpu as pltpu
from jax.sharding import PartitionSpec as P

F32 = jnp.float32
EXACT = lax.Precision.HIGHEST


def mm(a, b):
    return lax.dot_general(a, b, (((1,), (0,)), ((), ())), precision=EXACT, preferred_element_type=F32)


def mm_nt(a, b):
    return lax.dot_general(a, b, (((1,), (1,)), ((), ())), precision=EXACT, preferred_element_type=F32)


def low_lanes(shape):
    return lax.broadcasted_iota(jnp.int32, shape, 1) < shape[1] // 2


def swap(x):
    return pltpu.roll(x, x.shape[1] // 2, 1)


def inverse(a):
    n = a.shape[0]
    lane = lax.broadcasted_iota(jnp.int32, (8, 2 * n), 1)
    sub = lax.broadcasted_iota(jnp.int32, (8, 2 * n), 0)
    sign = jnp.where(lane < n, -1.0, 1.0).astype(F32)
    tiles = [a[8 * t : 8 * t + 8, :] for t in range(n // 8)]

    def col(x, c):
        return jnp.broadcast_to(x[:, c : c + 1], (8, 2 * n))

    def row(x, j):
        return jnp.broadcast_to(x[j : j + 1, :], (8, 2 * n))

    for kb in range(n // 8):
        k0 = 8 * kb
        dr = [col(tiles[kb], k0 + j) for j in range(8)]
        di = [col(tiles[kb], n + k0 + j) for j in range(8)]
        in_re = (lane >= k0) & (lane < k0 + 8)
        in_im = (lane >= n + k0) & (lane < n + k0 + 8)
        panel = jnp.where(in_re, jnp.where(sub == lane - k0, 1.0, 0.0), jnp.where(in_im, 0.0, tiles[kb]))
        turned = pltpu.roll(panel, n, 1) * sign
        others = [t for t in range(n // 8) if t != kb]
        cr = {t: [col(tiles[t], k0 + j) for j in range(8)] for t in others}
        ci = {t: [col(tiles[t], n + k0 + j) for j in range(8)] for t in others}
        for j in range(8):
            me = sub == j
            pr, pi = row(dr[j], j), row(di[j], j)
            size = 1.0 / (pr * pr + pi * pi)
            qr, qi = pr * size, -pi * size
            for m in range(j + 1, 8):
                ar, ai = row(dr[m], j), row(di[m], j)
                tr, ti = ar * qr - ai * qi, ar * qi + ai * qr
                dr[m], di[m] = (
                    jnp.where(me, tr, dr[m] - dr[j] * tr + di[j] * ti),
                    jnp.where(me, ti, di[m] - dr[j] * ti - di[j] * tr),
                )
            pj, tj = row(panel, j), row(turned, j)
            s, sx = pj * qr + tj * qi, tj * qr - pj * qi
            panel, turned = (
                jnp.where(me, s, panel - dr[j] * s - di[j] * sx),
                jnp.where(me, sx, turned - dr[j] * sx + di[j] * s),
            )
        tiles[kb] = panel
        rows = [row(panel, j) for j in range(8)]
        turns = [row(turned, j) for j in range(8)]
        for t in others:
            b = jnp.where(in_re | in_im, 0.0, tiles[t])
            for j in range(8):
                b = b - cr[t][j] * rows[j] - ci[t][j] * turns[j]
            tiles[t] = b
    return jnp.concatenate(tiles, axis=0)


def embed(a):
    low = low_lanes(a.shape)
    return jnp.concatenate([jnp.where(low, a, -a), swap(a)], axis=0)


def embed_pair(x):
    n = x.shape[0] // 2
    top, bot = x[:n], x[n:]
    low = low_lanes(top.shape)
    st, sb = swap(top), swap(bot)
    first = jnp.concatenate([jnp.where(low, top, -sb), jnp.where(low, bot, st)], axis=0)
    second = jnp.concatenate([jnp.where(low, st, -bot), jnp.where(low, sb, top)], axis=0)
    return first, second


def kernel_call(body, outs, *args, smem=0, name=None):
    spaces = [pltpu.VMEM] * (len(args) - smem) + [pltpu.SMEM] * smem
    return pl.pallas_call(
        body,
        out_shape=[jax.ShapeDtypeStruct(o, F32) for o in outs],
        in_specs=[pl.BlockSpec(memory_space=m) for m in spaces],
        out_specs=[pl.BlockSpec(memory_space=pltpu.VMEM)] * len(outs),
        name=name,
    )(*args)


def condense_body(g_ref, map_ref, rows_ref, sep_ref, pole_ref, vt_ref, k_ref):
    n = g_ref.shape[1]
    s = sep_ref.shape[0]
    spread = []
    for side in range(2):
        where = rows_ref[side : side + 1, :]
        hot = (lax.broadcasted_iota(jnp.int32, (n, where.shape[1]), 0) == where).astype(F32)
        spread.append(mm_nt(map_ref[side], hot))
    both = jnp.concatenate(spread, axis=0)
    ones = lax.broadcasted_iota(jnp.int32, (s, s), 0) == lax.broadcasted_iota(jnp.int32, (s, s), 1)
    for part in range(2):
        vt = mm(both, g_ref[part])
        vt_ref[2 * s * part : 2 * s * (part + 1), :] = vt
        k_ref[2 * s * part : 2 * s * (part + 1), :] = mm_nt(vt, both)
        shift = jnp.where(ones, pole_ref[part], 0.0)
        own = sep_ref[...] - shift if part == 0 else -shift
        k_ref[2 * s * part : 2 * s * part + s, :s] += own


def rights_body(vt_ref, y_ref, ysep_ref, r_ref):
    s = ysep_ref.shape[0]
    r_ref[...] = mm(vt_ref[...], y_ref[...])
    r_ref[:s, :] += ysep_ref[...]


def merge_body(mine_ref, his_ref, rm_ref, rh_ref, flag_ref, k_ref, r_ref, w_ref, v_ref):
    first = flag_ref[0] == 0
    s = k_ref.shape[0] // 4

    def pick(x, y):
        return jnp.where(first, x, y), jnp.where(first, y, x)

    ka, kb = pick(mine_ref[...], his_ref[...])
    ra, rb = pick(rm_ref[...], rh_ref[...])
    aer, afr, aei, afi = (ka[i * s : (i + 1) * s] for i in range(4))
    ber, bfr, bei, bfi = (kb[i * s : (i + 1) * s] for i in range(4))
    low = low_lanes((s, 2 * s))
    pivot = -jnp.where(low, aer + swap(bfr), swap(aei) + bfi)
    inv = embed(inverse(pivot))
    near = jnp.concatenate([jnp.where(low, bfr, aer), jnp.where(low, bfi, aei)], axis=0)
    right = jnp.concatenate([ra[:s] + rb[s : 2 * s], ra[2 * s : 3 * s] + rb[3 * s :]], axis=0)
    w, v = mm(inv, near), mm(inv, right)
    w_ref[...] = w
    v_ref[...] = v
    far = jnp.concatenate(
        [
            jnp.where(low, swap(ber), -bei),
            jnp.where(low, afr, -swap(afi)),
            jnp.where(low, swap(bei), ber),
            jnp.where(low, afi, swap(afr)),
        ],
        axis=0,
    )
    base = jnp.concatenate(
        [jnp.where(low, ber, 0.0), jnp.where(low, 0.0, afr), jnp.where(low, bei, 0.0), jnp.where(low, 0.0, afi)], axis=0
    )
    k_ref[...] = base + mm(far, w)
    rest = jnp.concatenate([rb[:s], ra[s : 2 * s], rb[2 * s : 3 * s], ra[3 * s :]], axis=0)
    r_ref[...] = rest + mm(far, v)


def open_body(k_ref, r_ref, kn_ref, rn_ref, flag_ref, p_ref, n_ref, q_ref, w_ref, v_ref):
    s = p_ref.shape[0]
    k, kn, r = k_ref[...], kn_ref[...], r_ref[...]
    er, ei = k[:s], k[2 * s : 3 * s]
    fr, fi = kn[:s], kn[s:]
    low = low_lanes((s, 2 * s))
    pivot = -jnp.where(low, er + swap(fr), swap(ei) + fi)
    left = jnp.where(flag_ref[0] == 0, 0.0, 1.0)
    near = jnp.concatenate([jnp.where(low, fr, er * left), jnp.where(low, fi, ei * left)], axis=0)
    right = jnp.concatenate([r[:s], r[2 * s : 3 * s]], axis=0) + rn_ref[...]
    inv = embed(inverse(pivot))
    p_ref[...] = pivot
    n_ref[...] = near
    q_ref[...] = right
    w_ref[...] = mm(inv, near)
    v_ref[...] = mm(inv, right)


def level_step(p_ref, n_ref, q_ref, wu_ref, vu_ref, wd_ref, vd_ref):
    s = p_ref.shape[0]
    up, down = embed_pair(n_ref[...])
    a, b = mm(up, wu_ref[...]), mm(down, wd_ref[...])
    low = low_lanes(a.shape)
    d = jnp.where(low, b, a)
    d = d + swap(d)
    pivot = p_ref[...] - jnp.where(low[:s], d[:s], d[s:])
    right = q_ref[...] + mm(up, vu_ref[...]) + mm(down, vd_ref[...])
    return pivot, jnp.where(low, a, b), right


def level_body(p_ref, n_ref, q_ref, wu_ref, vu_ref, wd_ref, vd_ref, po_ref, no_ref, qo_ref, w_ref, v_ref):
    pivot, near, right = level_step(p_ref, n_ref, q_ref, wu_ref, vu_ref, wd_ref, vd_ref)
    inv = embed(inverse(pivot))
    po_ref[...] = pivot
    no_ref[...] = near
    qo_ref[...] = right
    w_ref[...] = mm(inv, near)
    v_ref[...] = mm(inv, right)


def last_body(p_ref, n_ref, q_ref, wu_ref, vu_ref, wd_ref, vd_ref, s_ref):
    pivot, _, right = level_step(p_ref, n_ref, q_ref, wu_ref, vu_ref, wd_ref, vd_ref)
    s_ref[...] = mm(embed(inverse(pivot)), right)


def back_body(w_ref, v_ref, after_ref, before_ref, s_ref):
    one, two = embed_pair(w_ref[...])
    s_ref[...] = v_ref[...] + mm(one, after_ref[...]) + mm(two, before_ref[...])


def field_body(g_ref, vt_ref, y_ref, after_ref, before_ref, pole_ref, f_ref, fs_ref):
    s = fs_ref.shape[0]
    wr, wi = pole_ref[2], pole_ref[3]
    after, before, y = after_ref[...], before_ref[...], y_ref[...]
    real = [wr * x[:s] - wi * x[s:] for x in (after, before)]
    imag = [-wr * x[s:] - wi * x[:s] for x in (after, before)]
    fs_ref[...] = real[0]
    sol = jnp.concatenate(real + imag, axis=0)
    f_ref[...] = (
        mm(g_ref[0], wr * y)
        - mm(g_ref[1], wi * y)
        + lax.dot_general(vt_ref[...], sol, (((0,), (0,)), ((), ())), precision=EXACT, preferred_element_type=F32)
    )


def gather_rows(y, groups_z, groups_x):
    rows, cols = y.shape
    a = jnp.broadcast_to(y[None], (4, rows, cols))
    a = lax.all_to_all(a, "pole", 0, 0, tiled=True, axis_index_groups=groups_z)
    b = jnp.broadcast_to(a[None], (4, 4, rows, cols))
    b = lax.all_to_all(b, "pole", 0, 0, tiled=True, axis_index_groups=groups_x)
    return b.transpose(1, 0, 2, 3).reshape(16 * rows, cols)


def scatter_sum(field, sep, groups_z, groups_x):
    nf, ns, half = field.shape[0] // 16, sep.shape[0] // 16, field.shape[1] // 2
    f = field.reshape(4, 4, nf, 2, half).transpose(1, 0, 3, 2, 4).reshape(4, 4, 2 * nf, half)
    p = sep.reshape(4, 4, ns, 2, half).transpose(1, 0, 3, 2, 4).reshape(4, 4, 2 * ns, half)
    a = jnp.concatenate([f, p], axis=2)
    a = lax.all_to_all(a, "pole", 0, 0, tiled=True, axis_index_groups=groups_x).sum(0)
    a = lax.all_to_all(a, "pole", 0, 0, tiled=True, axis_index_groups=groups_z).sum(0)
    f = a[: 2 * nf].reshape(2, nf, half).transpose(1, 0, 2).reshape(nf, 2 * half)
    p = a[2 * nf :].reshape(2, ns, half).transpose(1, 0, 2).reshape(ns, 2 * half)
    return f, p


def hop(x, pairs):
    return lax.ppermute(x, "dom", pairs)


def shards(y_interior, y_separator, green, pole_data, coupling, sep_block, iface_rows):
    poles, doms = lax.axis_size("pole"), lax.axis_size("dom")
    g = green[:, 0, 0]
    pole = pole_data[:, 0]
    s, cols = y_separator.shape[1], y_separator.shape[2]
    groups_z = [[x + 4 * z for z in range(4)] for x in range(4)]
    groups_x = [[x + 4 * z for x in range(4)] for z in range(4)]
    y = y_interior[0] if poles == 1 else gather_rows(y_interior[0], groups_z, groups_x)
    me = lax.axis_index("dom")
    core, side, line = me % 2, (me // 2) % 2, me // 4
    core_flag, side_flag, line_flag = (v.astype(jnp.int32)[None] for v in (core, side, line))
    swap_core = [(i, i ^ 1) for i in range(doms)]
    swap_side = [(i, i ^ 2) for i in range(doms)]

    def shift(k):
        return [(i, i + k) for i in range(max(0, -k), doms - max(0, k))]

    vt, k0 = kernel_call(
        condense_body, [(4 * s, g.shape[1]), (4 * s, 2 * s)], g, coupling[0], iface_rows[0], sep_block[0], pole, smem=1, name="condense"
    )
    (r0,) = kernel_call(rights_body, [(4 * s, cols)], vt, y, y_separator[0], name="rights")

    half = cols // 2
    mine = jnp.where(core == 0, r0[:, :half], r0[:, half:])
    sent = jnp.where(core == 0, r0[:, half:], r0[:, :half])
    got = hop(jnp.concatenate([k0, sent], axis=1), swap_core)
    k1, r1, w1, v1 = kernel_call(
        merge_body, [(4 * s, 2 * s), (4 * s, half), (2 * s, 2 * s), (2 * s, half)],
        k0, got[:, : 2 * s], mine, got[:, 2 * s :], core_flag, smem=1, name="merge_core",
    )

    quarter = half // 2
    mine = jnp.where(side == 0, r1[:, :quarter], r1[:, quarter:])
    sent = jnp.where(side == 0, r1[:, quarter:], r1[:, :quarter])
    k_part = jnp.where(core == 0, k1[: 2 * s], k1[2 * s :])
    got = hop(jnp.concatenate([k_part, jnp.concatenate([sent[: 2 * s], sent[2 * s :]], axis=1)], axis=0), swap_side)
    other = hop(got[: 2 * s], swap_core)
    k_his = jnp.concatenate(
        [jnp.where(core == 0, got[: 2 * s], other), jnp.where(core == 0, other, got[: 2 * s])], axis=0
    )
    r_his = jnp.concatenate([got[2 * s :, :quarter], got[2 * s :, quarter:]], axis=0)
    k2, r2, w2, v2 = kernel_call(
        merge_body, [(4 * s, 2 * s), (4 * s, quarter), (2 * s, 2 * s), (2 * s, quarter)],
        k1, k_his, mine, r_his, side_flag, smem=1, name="merge_side",
    )

    k_before = jnp.concatenate([k2[s : 2 * s], k2[3 * s :]], axis=0)
    r_before = jnp.concatenate([r2[s : 2 * s], r2[3 * s :]], axis=0)
    got = hop(jnp.concatenate([k_before, r_before], axis=1), shift(-4))
    sizes = [(s, 2 * s), (2 * s, 2 * s), (2 * s, quarter), (2 * s, 2 * s), (2 * s, quarter)]
    p, n, q, w, v = kernel_call(
        open_body, sizes, k2, r2, got[:, : 2 * s], got[:, 2 * s :], line_flag, smem=1, name="open"
    )
    stride = 4
    while True:
        pack = jnp.concatenate([w, v], axis=1)
        up, down = hop(pack, shift(-stride)), hop(pack, shift(stride))
        args = (p, n, q, up[:, : 2 * s], up[:, 2 * s :], down[:, : 2 * s], down[:, 2 * s :])
        stride *= 2
        if stride >= doms:
            break
        p, n, q, w, v = kernel_call(level_body, sizes, *args, name="level")
    (after,) = kernel_call(last_body, [(2 * s, quarter)], *args, name="last")
    before = hop(after, shift(4))

    (middle,) = kernel_call(back_body, [(2 * s, quarter)], w2, v2, after, before, name="back_side")
    left, right = jnp.concatenate([middle, before], axis=1), jnp.concatenate([after, middle], axis=1)
    mine, sent = jnp.where(side == 0, left, right), jnp.where(side == 0, right, left)
    got = hop(sent, swap_side)
    after, before = (
        jnp.where(side == 0, jnp.concatenate([a, b], axis=1), jnp.concatenate([b, a], axis=1))
        for a, b in ((mine[:, :quarter], got[:, :quarter]), (mine[:, quarter:], got[:, quarter:]))
    )
    (middle,) = kernel_call(back_body, [(2 * s, half)], w1, v1, after, before, name="back_core")
    left, right = jnp.concatenate([middle, before], axis=1), jnp.concatenate([after, middle], axis=1)
    mine, sent = jnp.where(core == 0, left, right), jnp.where(core == 0, right, left)
    got = hop(sent, swap_core)
    after, before = (
        jnp.where(core == 0, jnp.concatenate([a, b], axis=1), jnp.concatenate([b, a], axis=1))
        for a, b in ((mine[:, :half], got[:, :half]), (mine[:, half:], got[:, half:]))
    )
    field, sep = kernel_call(
        field_body, [(g.shape[1], cols), (s, cols)], g, vt, y, after, before, pole, smem=1, name="field"
    )
    if poles > 1:
        field, sep = scatter_sum(field, sep, groups_z, groups_x)
    return field[None], sep[None]


def solution(mesh):
    return jax.shard_map(
        shards,
        mesh=mesh,
        in_specs=(
            P("dom", "pole", None),
            P("dom", None, None),
            P(None, "pole", "dom", None, None),
            P(None, "pole"),
            P("dom", None, None, None),
            P("dom", None, None),
            P("dom", None, None),
        ),
        out_specs=(P("dom", "pole", None), P("dom", "pole", None)),
        check_vma=False,
    )
```

```python
import jax
import jax.numpy as jnp
from jax import lax
from jax.experimental import pallas as pl
from jax.experimental.pallas import tpu as pltpu
from jax.sharding import PartitionSpec as P


F32 = jnp.float32
EXACT = lax.Precision.HIGHEST


def mm(a, b):
    return lax.dot_general(a, b, (((1,), (0,)), ((), ())), precision=EXACT, preferred_element_type=F32)


def mm_nt(a, b):
    return lax.dot_general(a, b, (((1,), (1,)), ((), ())), precision=EXACT, preferred_element_type=F32)


def low_lanes(shape):
    return lax.broadcasted_iota(jnp.int32, shape, 1) < shape[1] // 2


def swap(x):
    return pltpu.roll(x, x.shape[1] // 2, 1)


def inverse(a):
    n = a.shape[0]
    lane = lax.broadcasted_iota(jnp.int32, (8, 2 * n), 1)
    sub = lax.broadcasted_iota(jnp.int32, (8, 2 * n), 0)
    sign = jnp.where(lane < n, -1.0, 1.0).astype(F32)
    tiles = [a[8 * t : 8 * t + 8, :] for t in range(n // 8)]

    def col(x, c):
        return jnp.broadcast_to(x[:, c : c + 1], (8, 2 * n))

    def row(x, j):
        return jnp.broadcast_to(x[j : j + 1, :], (8, 2 * n))

    for kb in range(n // 8):
        k0 = 8 * kb
        dr = [col(tiles[kb], k0 + j) for j in range(8)]
        di = [col(tiles[kb], n + k0 + j) for j in range(8)]
        in_re = (lane >= k0) & (lane < k0 + 8)
        in_im = (lane >= n + k0) & (lane < n + k0 + 8)
        panel = jnp.where(in_re, jnp.where(sub == lane - k0, 1.0, 0.0), jnp.where(in_im, 0.0, tiles[kb]))
        turned = pltpu.roll(panel, n, 1) * sign
        others = [t for t in range(n // 8) if t != kb]
        cr = {t: [col(tiles[t], k0 + j) for j in range(8)] for t in others}
        ci = {t: [col(tiles[t], n + k0 + j) for j in range(8)] for t in others}
        for j in range(8):
            me = sub == j
            pr, pi = row(dr[j], j), row(di[j], j)
            size = 1.0 / (pr * pr + pi * pi)
            qr, qi = pr * size, -pi * size
            for m in range(j + 1, 8):
                ar, ai = row(dr[m], j), row(di[m], j)
                tr, ti = ar * qr - ai * qi, ar * qi + ai * qr
                dr[m], di[m] = (
                    jnp.where(me, tr, dr[m] - dr[j] * tr + di[j] * ti),
                    jnp.where(me, ti, di[m] - dr[j] * ti - di[j] * tr),
                )
            pj, tj = row(panel, j), row(turned, j)
            s, sx = pj * qr + tj * qi, tj * qr - pj * qi
            panel, turned = (
                jnp.where(me, s, panel - dr[j] * s - di[j] * sx),
                jnp.where(me, sx, turned - dr[j] * sx + di[j] * s),
            )
        tiles[kb] = panel
        rows = [row(panel, j) for j in range(8)]
        turns = [row(turned, j) for j in range(8)]
        for t in others:
            b = jnp.where(in_re | in_im, 0.0, tiles[t])
            for j in range(8):
                b = b - cr[t][j] * rows[j] - ci[t][j] * turns[j]
            tiles[t] = b
    return jnp.concatenate(tiles, axis=0)


def embed(a):
    low = low_lanes(a.shape)
    return jnp.concatenate([jnp.where(low, a, -a), swap(a)], axis=0)


def embed_pair(x):
    n = x.shape[0] // 2
    top, bot = x[:n], x[n:]
    low = low_lanes(top.shape)
    st, sb = swap(top), swap(bot)
    first = jnp.concatenate([jnp.where(low, top, -sb), jnp.where(low, bot, st)], axis=0)
    second = jnp.concatenate([jnp.where(low, st, -bot), jnp.where(low, sb, top)], axis=0)
    return first, second


def kernel_call(body, outs, *args, smem=0, us=1.0, loose=(), loose_outs=False, hbm=(), scratch=()):
    count = len(args) - smem
    args = [
        a
        if i >= count or i in loose
        else pltpu.with_memory_space_constraint(a, pltpu.HBM if i in hbm else pltpu.VMEM)
        for i, a in enumerate(args)
    ]
    return pl.pallas_call(
        body,
        out_shape=[jax.ShapeDtypeStruct(o, F32) if loose_outs else pltpu.VMEM(o, F32) for o in outs],
        cost_estimate=pl.CostEstimate(flops=int(us * 1e9), bytes_accessed=1 << 16, transcendentals=0),
        in_specs=[
            pl.BlockSpec(memory_space=pltpu.SMEM if i >= count else pltpu.HBM if i in hbm else pltpu.VMEM)
            for i in range(len(args))
        ],
        scratch_shapes=list(scratch),
        out_specs=[pl.BlockSpec(memory_space=pltpu.VMEM)] * len(outs),
        compiler_params=pltpu.CompilerParams(vmem_limit_bytes=16 << 20),
    )(*args)


def condense_body(g_hbm, map_hbm, sep_hbm, rows_ref, pole_ref, vt_ref, k_ref, g_ref, map_ref, sep_ref, sems):
    moves = [
        pltpu.make_async_copy(map_hbm, map_ref, sems.at[0]),
        pltpu.make_async_copy(g_hbm.at[0], g_ref.at[0], sems.at[1]),
        pltpu.make_async_copy(g_hbm.at[1], g_ref.at[1], sems.at[2]),
        pltpu.make_async_copy(sep_hbm, sep_ref, sems.at[3]),
    ]
    for move in moves:
        move.start()
    n = g_ref.shape[1]
    s = sep_ref.shape[0]
    spread = []
    moves[0].wait()
    for side in range(2):
        where = rows_ref[side : side + 1, :]
        hot = (lax.broadcasted_iota(jnp.int32, (n, where.shape[1]), 0) == where).astype(F32)
        spread.append(mm_nt(map_ref[side], hot))
    both = jnp.concatenate(spread, axis=0)
    ones = lax.broadcasted_iota(jnp.int32, (s, s), 0) == lax.broadcasted_iota(jnp.int32, (s, s), 1)
    for part in range(2):
        moves[1 + part].wait()
        vt = mm(both, g_ref[part])
        vt_ref[2 * s * part : 2 * s * (part + 1), :] = vt
        k_ref[2 * s * part : 2 * s * (part + 1), :] = mm_nt(vt, both)
    moves[3].wait()
    for part in range(2):
        shift = jnp.where(ones, pole_ref[part], 0.0)
        own = sep_ref[...] - shift if part == 0 else -shift
        k_ref[2 * s * part : 2 * s * part + s, :s] += own


def in_order(y_ref):
    return jnp.concatenate([y_ref[x, z] for z in range(y_ref.shape[1]) for x in range(y_ref.shape[0])], axis=0)


def rights_body(vt_ref, y_ref, ysep_ref, flag_ref, mine_ref, sent_ref):
    s, half = ysep_ref.shape[0], mine_ref.shape[1]
    r = mm(vt_ref[...], in_order(y_ref))
    r = jnp.concatenate([r[:s] + ysep_ref[...], r[s:]], axis=0)
    first = flag_ref[0] == 0
    mine_ref[...] = jnp.where(first, r[:, :half], r[:, half:])
    sent_ref[...] = jnp.where(first, r[:, half:], r[:, :half])


def join_matrices(first, ka, kb):
    s = ka.shape[0] // 4
    ka, kb = jnp.where(first, ka, kb), jnp.where(first, kb, ka)
    aer, afr, aei, afi = (ka[i * s : (i + 1) * s] for i in range(4))
    ber, bfr, bei, bfi = (kb[i * s : (i + 1) * s] for i in range(4))
    low = low_lanes((s, 2 * s))
    inv = embed(inverse(-jnp.where(low, aer + swap(bfr), swap(aei) + bfi)))
    near = jnp.concatenate([jnp.where(low, bfr, aer), jnp.where(low, bfi, aei)], axis=0)
    far = jnp.concatenate(
        [
            jnp.where(low, swap(ber), -bei),
            jnp.where(low, afr, -swap(afi)),
            jnp.where(low, swap(bei), ber),
            jnp.where(low, afi, swap(afr)),
        ],
        axis=0,
    )
    base = jnp.concatenate(
        [jnp.where(low, ber, 0.0), jnp.where(low, 0.0, afr), jnp.where(low, bei, 0.0), jnp.where(low, 0.0, afi)], axis=0
    )
    w = mm(inv, near)
    return base + mm(far, w), w, inv, far


def core_join_body(mine_ref, his_ref, core_ref, k_ref, part_ref, w_ref, inv_ref, far_ref):
    lead = core_ref[0] == 0
    k, w_ref[...], inv_ref[...], far_ref[...] = join_matrices(lead, mine_ref[...], his_ref[...])
    half = k.shape[0] // 2
    k_ref[...] = k
    part_ref[...] = jnp.where(lead, k[:half], k[half:])


def side_join_body(mine_ref, one_ref, two_ref, core_ref, flag_ref, k_ref, w_ref, inv_ref, far_ref):
    lead = core_ref[0] == 0
    one, two = one_ref[...], two_ref[...]
    his = jnp.concatenate([jnp.where(lead, one, two), jnp.where(lead, two, one)], axis=0)
    k_ref[...], w_ref[...], inv_ref[...], far_ref[...] = join_matrices(flag_ref[0] == 0, mine_ref[...], his)


def join_body(mine_ref, his_ref, flag_ref, k_ref, w_ref, inv_ref, far_ref):
    k_ref[...], w_ref[...], inv_ref[...], far_ref[...] = join_matrices(flag_ref[0] == 0, mine_ref[...], his_ref[...])


def sides_body(mine_ref, his_ref, inv_ref, far_ref, flag_ref, r_ref, v_ref):
    s = mine_ref.shape[0] // 4
    first = flag_ref[0] == 0
    mine, his = mine_ref[...], his_ref[...]
    ra, rb = jnp.where(first, mine, his), jnp.where(first, his, mine)
    v = mm(inv_ref[...], jnp.concatenate([ra[:s] + rb[s : 2 * s], ra[2 * s : 3 * s] + rb[3 * s :]], axis=0))
    v_ref[...] = v
    rest = jnp.concatenate([rb[:s], ra[s : 2 * s], rb[2 * s : 3 * s], ra[3 * s :]], axis=0)
    r_ref[...] = rest + mm(far_ref[...], v)


def end_body(k_ref, flag_ref, sent_ref, inv_ref, back_ref, fore_ref):
    s = sent_ref.shape[0]
    er, fr, ei, fi = (k_ref[i * s : (i + 1) * s, :] for i in range(4))
    low = low_lanes((s, 2 * s))
    ee = jnp.where(low, er, swap(ei))
    inv = embed(inverse(-ee))
    fore = embed(jnp.where(low, swap(er), ei))
    back = embed(jnp.where(low, fr, swap(fi)))
    inv_ref[...] = inv
    back_ref[...] = back
    through = mm(inv, fore)
    fore_ref[...] = through
    ff = jnp.where(low, swap(fr), fi)
    more = mm(back[:s], through)
    sent_ref[...] = jnp.where(flag_ref[0] == 0, ee, ff + jnp.where(low, more, -more))


def end_sides_body(r_ref, inv_ref, back_ref, flag_ref, sent_ref, v_ref):
    s = r_ref.shape[0] // 4
    e = jnp.concatenate([r_ref[:s, :], r_ref[2 * s : 3 * s, :]], axis=0)
    f = jnp.concatenate([r_ref[s : 2 * s, :], r_ref[3 * s :, :]], axis=0)
    v = mm(inv_ref[...], e)
    v_ref[...] = v
    sent_ref[...] = jnp.where(flag_ref[0] == 0, e, f + mm(back_ref[...], v))


def middle_body(mine_ref, his_ref, inv_ref):
    inv_ref[...] = embed(inverse(-(mine_ref[...] + his_ref[...])))


def back_body(*refs):
    inv_ref, mine_ref, his_ref, fore_ref, v_ref = refs[:5]
    flags, (own_ref, sent_ref) = refs[-3], refs[-2:]
    joins = refs[5:-3]
    s2 = v_ref.shape[0]
    middle = mm(inv_ref[...], mine_ref[...] + his_ref[...])
    front = flags[4] == 0
    after = jnp.where(front, middle, v_ref[...] + mm(fore_ref[...], middle))
    before = jnp.where(front, 0.0, middle)
    for level in range(3, -1, -1):
        one, two = embed_pair(joins[2 * level][...])
        middle = joins[2 * level + 1][...] + mm(
            jnp.concatenate([one, two], axis=1), jnp.concatenate([after, before], axis=0)
        )
        first = flags[level] == 0
        if level == 0:
            sent_ref[:s2, :] = jnp.where(first, after, middle)
            sent_ref[s2:, :] = jnp.where(first, middle, before)
        after, before = jnp.where(first, middle, after), jnp.where(first, before, middle)
    own_ref[:s2, :] = after
    own_ref[s2:, :] = before


def base_body(g_ref, y_ref, pole_ref, a_ref):
    y = in_order(y_ref)
    a_ref[...] = mm(g_ref[0], pole_ref[2] * y) - mm(g_ref[1], pole_ref[3] * y)


def field_body(base_ref, vt_ref, mine_ref, got_ref, pole_ref, core_ref, o_ref):
    s = mine_ref.shape[0] // 4
    wr, wi = pole_ref[2], pole_ref[3]
    lead = core_ref[0] == 0
    mine, got = mine_ref[...], got_ref[...]
    x = jnp.concatenate([jnp.where(lead, mine, got), jnp.where(lead, got, mine)], axis=1)
    re, im = [x[:s], x[2 * s : 3 * s]], [x[s : 2 * s], x[3 * s :]]
    real = [wr * a - wi * b for a, b in zip(re, im)]
    imag = [-wr * b - wi * a for a, b in zip(re, im)]
    sol = jnp.concatenate(real + imag, axis=0)
    field = base_ref[...] + lax.dot_general(
        vt_ref[...], sol, (((0,), (0,)), ((), ())), precision=EXACT, preferred_element_type=F32
    )
    nx, nz = o_ref.shape[:2]
    nf, ns, half = field.shape[0] // (nx * nz), s // (nx * nz), field.shape[1] // 2
    for i in range(nx * nz):
        z, x = divmod(i, nx)
        for h in range(2):
            o_ref[x, z, h * nf : (h + 1) * nf, :] = field[i * nf : (i + 1) * nf, h * half : (h + 1) * half]
            at = 2 * nf + h * ns
            o_ref[x, z, at : at + ns, :] = real[0][i * ns : (i + 1) * ns, h * half : (h + 1) * half]


def close_body(a_ref, f_ref, s_ref):
    a = a_ref[0]
    for i in range(1, a_ref.shape[0]):
        a = a + a_ref[i]
    nf, ns, half = f_ref.shape[0], s_ref.shape[0], a.shape[1]
    for h in range(2):
        f_ref[:, h * half : (h + 1) * half] = a[h * nf : (h + 1) * nf, :]
        s_ref[:, h * half : (h + 1) * half] = a[2 * nf + h * ns : 2 * nf + (h + 1) * ns, :]


def shards(y_interior, y_separator, green, pole_data, coupling, sep_block, iface_rows):
    doms = lax.axis_size("dom")
    g = green[:, 0, 0]
    pole = pole_data[:, 0]
    s, cols = y_separator.shape[1], y_separator.shape[2]
    rows = y_interior.shape[1]
    half = cols // 2
    groups_z = [[x + 4 * z for z in range(4)] for x in range(4)]
    groups_x = [[x + 4 * z for x in range(4)] for z in range(4)]

    def flip(x, k):
        return lax.ppermute(x, "dom", [(i, i ^ k) for i in range(doms)])

    def exchange(a, groups):
        return lax.all_to_all(a, "pole", 0, 0, tiled=True, axis_index_groups=groups)

    y = exchange(jnp.broadcast_to(y_interior[0][None], (4, rows, cols)), groups_z)
    y = exchange(jnp.broadcast_to(y[None], (4, 4, rows, cols)), groups_x)
    me = lax.axis_index("dom").astype(jnp.int32)
    flags = jnp.stack([(me >> i) & 1 for i in range(5)])
    core = flags[:1]

    big, square = (4 * s, 2 * s), (2 * s, 2 * s)
    vt, k = kernel_call(
        condense_body, [(4 * s, g.shape[1]), big], g, coupling[0], sep_block[0], iface_rows[0], pole,
        smem=1, us=3.0, loose=(3,), hbm=(0, 1, 2),
        scratch=[pltpu.VMEM(a, F32) for a in (g.shape, coupling.shape[1:], (s, s))] + [pltpu.SemaphoreType.DMA((4,))],
    )
    outs = [big, square, square, big]
    k, part, w, inv, far = kernel_call(
        core_join_body, [big] + outs[1:2] + outs[1:], k, flip(k, 1), core, smem=1, us=3.5
    )
    joins = [(w, inv, far)]
    one = flip(part, 2)
    k, w, inv, far = kernel_call(side_join_body, outs, k, one, flip(one, 1), core, flags[1:2], smem=2, us=3.5)
    joins.append((w, inv, far))
    for level in range(2, 4):
        his = flip(k, 1 << level)
        k, w, inv, far = kernel_call(join_body, outs, k, his, flags[level : level + 1], smem=1, us=3.5)
        joins.append((w, inv, far))
    k_end, inv_end, back, fore = kernel_call(end_body, [(s, 2 * s)] + [square] * 3, k, flags[4:], smem=1, us=3.5)
    (inv_mid,) = kernel_call(middle_body, [square], k_end, flip(k_end, 16), us=3.5)

    (base,) = kernel_call(base_body, [(g.shape[1], cols)], g, y, pole, smem=1, us=2.0, loose_outs=True)
    r, sent = kernel_call(rights_body, [(4 * s, half)] * 2, vt, y, y_separator[0], core, smem=1, us=0.7, loose=(2,))
    solved = []
    for level, (w, inv, far) in enumerate(joins):
        his = flip(sent if level == 0 else r, 1 << level)
        r, v = kernel_call(
            sides_body, [(4 * s, half), (2 * s, half)], r, his, inv, far, flags[level : level + 1],
            smem=1, us=0.5,
        )
        solved += [w, v]
    r_end, v_end = kernel_call(end_sides_body, [(2 * s, half)] * 2, r, inv_end, back, flags[4:], smem=1, us=0.4)
    own, sent = kernel_call(
        back_body, [(4 * s, half)] * 2, inv_mid, r_end, flip(r_end, 16), fore, v_end, *solved, flags,
        smem=1, us=1.5,
    )
    (total,) = kernel_call(
        field_body, [(4, 4, 2 * rows + s // 8, half)], base, vt, own, flip(sent, 1), pole, core,
        smem=2, loose=(0,),
    )
    total = exchange(total, groups_x).sum(0)
    total = exchange(total, groups_z)
    field, sep = kernel_call(close_body, [(rows, cols), (s // 16, cols)], total, us=0.2, loose_outs=True)
    return field[None], sep[None]


def solution(mesh):
    return jax.shard_map(
        shards,
        mesh=mesh,
        in_specs=(
            P("dom", "pole", None),
            P("dom", None, None),
            P(None, "pole", "dom", None, None),
            P(None, "pole"),
            P("dom", None, None, None),
            P("dom", None, None),
            P("dom", None, None),
        ),
        out_specs=(P("dom", "pole", None), P("dom", "pole", None)),
        check_vma=False,
    )
```
